32 devices in a mesh: mem: 4 (over y, x), sp: 8 (over z, core).
Axes of the slice: x: 2, y: 2, z: 4, core: 2. Of those that a mesh axis runs over, the one named last changes fastest.
Arguments:
- member_predictors: bfloat16 [32, 8, 16, 128], P('mem', None, 'sp'), may hold values from -6 to 6
- member_skill_logit: bfloat16 [32, 16, 128], P('mem', 'sp'), may hold values from -8 to 250
- opening_filter: bfloat16 [9, 8, 128], replicated, may hold values from -0.75 to 0.75
- opening_bias: float32 [128], replicated, may hold values from -3 to 3
- following_filter: bfloat16 [9, 128, 128], replicated, may hold values from -0.1875 to 0.1875
- layer_norm_scales: float32 [2, 2, 128], replicated, may hold values from 0.5 to 1.5
- query_key_value_weight: bfloat16 [2, 128, 384], replicated, may hold values from -0.5 to 0.5
- attention_output_weight: bfloat16 [2, 128, 128], replicated, may hold values from -0.5 to 0.5
- upward_weight: bfloat16 [2, 128, 512], replicated, may hold values from -0.5 to 0.5
- downward_weight: bfloat16 [2, 512, 128], replicated, may hold values from -0.25 to 0.25
- closing_norm_scale: float32 [128], replicated, may hold values from 0.5 to 1.5
- readout_weight: bfloat16 [128, 2], replicated, may hold values from -0.5 to 0.5
Outputs:
- corrected: float32 [32, 2, 16, 128], P('mem', None, 'sp')
The draws below stay inside these ranges and needn't reach their ends.
All inputs are finite; a program needn't handle non-finite values.
Results may differ from the reference program's by a relative error of at most 0.012.
Values may be sent and summed in bfloat16 or wider, within the bound.
A program may use at most 64 MiB of HBM per device.

```python
import math
import jax
import jax.numpy as jnp
from jax import lax

PREDICTOR_COUNT = 8
CORRECTED_COUNT = 2
E = 128
HEADS = 8
FF = 512
LAYERS = 2
GRID_COLUMNS = 128
MEMBER_COUNT = 32
GRID_ROWS = 16


def draw_member_skill_logit(key, part):
    baseline = jnp.clip(1.5 * jax.random.normal(jax.random.fold_in(key, 11), (MEMBER_COUNT, GRID_ROWS, GRID_COLUMNS), jnp.float32), -8.0, 8.0)
    return baseline.astype(jnp.bfloat16)


def level_of(key, extent, cuts, least, high):
    level = 1.0
    for axis_at, shards_of in cuts:
        steps = jax.random.uniform(jax.random.fold_in(jax.random.fold_in(key, 6), axis_at), (shards_of,), jnp.float32, least / len(cuts), high / len(cuts))
        level = level * jnp.repeat(jnp.exp(steps), extent[axis_at] // shards_of).reshape((-1,) + (1,) * (len(extent) - 1 - axis_at))
    return level


def gaussian(key, extent, deviation, reach, pieces=(), dtype=jnp.bfloat16):
    entries = jax.random.normal(key, extent, jnp.float32) * deviation
    if len(pieces) > 0:
        entries = level_of(key, extent, pieces, -0.22, 0.18) * entries
    return jnp.clip(entries, min=-reach, max=reach).astype(dtype)


def setup_inputs(seed: int = 0) -> dict:
    key_list = jax.random.split(jax.random.key(seed), 13)
    return {
        "member_predictors": gaussian(key_list[0], (MEMBER_COUNT, PREDICTOR_COUNT, GRID_ROWS, GRID_COLUMNS), 1.0, 6.0, ((0, 4), (2, 8))),
        "member_skill_logit": draw_member_skill_logit(jax.random.fold_in(key_list[12], 71), 0),
        "opening_filter": gaussian(key_list[2], (9, PREDICTOR_COUNT, E), (9 * PREDICTOR_COUNT) ** -0.5, 0.75),
        "opening_bias": gaussian(key_list[3], (E,), 0.5, 3.0, (), jnp.float32),
        "following_filter": gaussian(key_list[4], (9, E, E), (9 * E) ** -0.5, 0.1875),
        "layer_norm_scales": jnp.clip(1.0 + 0.1 * jax.random.normal(key_list[5], (LAYERS, 2, E), jnp.float32), 0.5, 1.5),
        "query_key_value_weight": gaussian(key_list[6], (LAYERS, E, 3 * E), E ** -0.5, 0.5),
        "attention_output_weight": gaussian(key_list[7], (LAYERS, E, E), E ** -0.5, 0.5),
        "upward_weight": gaussian(key_list[8], (LAYERS, E, FF), E ** -0.5, 0.5),
        "downward_weight": gaussian(key_list[9], (LAYERS, FF, E), FF ** -0.5, 0.25),
        "closing_norm_scale": jnp.clip(1.0 + 0.1 * jax.random.normal(key_list[10], (E,), jnp.float32), 0.5, 1.5),
        "readout_weight": gaussian(key_list[11], (E, CORRECTED_COUNT), E ** -0.5, 0.5),
    }


def layer_norm(stream, scaling):
    average = lax.optimization_barrier(jnp.mean(stream, -1, keepdims=True))
    centred = stream - average
    variance = lax.optimization_barrier(jnp.mean(centred * centred, -1, keepdims=True))
    return centred * lax.rsqrt(variance + 1e-05) * scaling

def conv_fields(border_padded, kernel):
    row_count = border_padded.shape[2] - 2
    col_count = border_padded.shape[3] - 2
    summed = jnp.zeros((border_padded.shape[0], row_count, col_count, kernel.shape[2]), jnp.float32)
    for stencil in range(9):
        row_off = stencil // 3
        col_off = stencil % 3
        shifted = border_padded[:, :, row_off:row_off + row_count, col_off:col_off + col_count]
        summed = summed + jnp.einsum('mchw,ce->mhwe', shifted.astype(jnp.float32), kernel[stencil].astype(jnp.float32))
    return summed

def conv_features(border_padded, kernel):
    row_count = border_padded.shape[1] - 2
    col_count = border_padded.shape[2] - 2
    summed = jnp.zeros((border_padded.shape[0], row_count, col_count, kernel.shape[2]), jnp.float32)
    for stencil in range(9):
        row_off = stencil // 3
        col_off = stencil % 3
        shifted = border_padded[:, row_off:row_off + row_count, col_off:col_off + col_count, :]
        summed = summed + jnp.einsum('mhwe,ef->mhwf', shifted.astype(jnp.float32), kernel[stencil].astype(jnp.float32))
    return summed

def members_attend(stream, logits, layer_norm_scales, query_key_value_weight, attention_output_weight, upward_weight, downward_weight, closing_norm_scale, readout_weight):
    blocks, members, width = stream.shape
    head_size = width // HEADS
    for layer in range(LAYERS):
        normed = layer_norm(stream, layer_norm_scales[layer, 0]).astype(jnp.bfloat16)
        triple = jnp.dot(normed.reshape(-1, width), query_key_value_weight[layer], preferred_element_type=jnp.float32).astype(jnp.bfloat16)
        triple = triple.reshape(blocks, members, 3, HEADS, head_size)
        queries = triple[:, :, 0].astype(jnp.float32)
        keys = triple[:, :, 1].astype(jnp.float32)
        values = triple[:, :, 2].astype(jnp.float32)
        scores = jnp.einsum('bqhd,bkhd->bhqk', queries, keys) / math.sqrt(head_size)
        scores = scores + logits.astype(jnp.float32)[:, None, None, :]
        highest = lax.optimization_barrier(jnp.max(scores, -1, keepdims=True))
        raised = jnp.exp(scores - highest)
        weights = (raised / lax.optimization_barrier(jnp.sum(raised, -1, keepdims=True))).astype(jnp.bfloat16)
        attended = jnp.einsum('bhqk,bkhd->bqhd', weights.astype(jnp.float32), values).astype(jnp.bfloat16)
        stream = stream + jnp.dot(attended.reshape(-1, width), attention_output_weight[layer], preferred_element_type=jnp.float32).reshape(blocks, members, width)
        normed = layer_norm(stream, layer_norm_scales[layer, 1]).astype(jnp.bfloat16)
        hidden = jax.nn.gelu(jnp.dot(normed.reshape(-1, width), upward_weight[layer], preferred_element_type=jnp.float32)).astype(jnp.bfloat16)
        stream = stream + jnp.dot(hidden, downward_weight[layer], preferred_element_type=jnp.float32).reshape(blocks, members, width)
    final = layer_norm(stream, closing_norm_scale).astype(jnp.bfloat16)
    return jnp.dot(final.reshape(-1, width), readout_weight, preferred_element_type=jnp.float32).reshape(blocks, members, readout_weight.shape[1])

def reference(member_predictors, member_skill_logit, opening_filter, opening_bias, following_filter, layer_norm_scales, query_key_value_weight, attention_output_weight, upward_weight, downward_weight, closing_norm_scale, readout_weight):

    def embed_member_fields(member_fields):
        border_padded = jnp.pad(member_fields, ((0, 0), (1, 1), (1, 1)))[None]
        first = jax.nn.gelu(conv_fields(border_padded, opening_filter) + opening_bias).astype(jnp.bfloat16)
        padded_first = jnp.pad(first, ((0, 0), (1, 1), (1, 1), (0, 0)))
        summed = first.astype(jnp.float32) + conv_features(padded_first, following_filter)
        return summed.astype(jnp.bfloat16)[0]
    member_features = lax.map(embed_member_fields, member_predictors)
    members = member_features.shape[0]
    cells = GRID_ROWS * GRID_COLUMNS
    block = math.gcd(cells, 64)
    stream = member_features.transpose(1, 2, 0, 3).reshape(cells // block, block, members, E)
    logit_blocks = member_skill_logit.transpose(1, 2, 0).reshape(cells // block, block, members)

    def one_block(packed):
        return members_attend(packed[0].astype(jnp.float32), packed[1], layer_norm_scales, query_key_value_weight, attention_output_weight, upward_weight, downward_weight, closing_norm_scale, readout_weight)
    field_adjustment = lax.map(one_block, (stream, logit_blocks))
    field_adjustment = field_adjustment.reshape(GRID_ROWS, GRID_COLUMNS, members, CORRECTED_COUNT).transpose(2, 3, 0, 1)
    return member_predictors[:, :CORRECTED_COUNT].astype(jnp.float32) + field_adjustment
```

```python
import functools
import math

import jax
import jax.numpy as jnp
from jax import lax
from jax.experimental import pallas as pl
from jax.experimental.pallas import tpu as pltpu
from jax.sharding import PartitionSpec as P

CORRECTED_COUNT = 2
HEADS = 8
LAYERS = 2
LANES = 128
BLOCK = 256


def extended(cells, axis, dim, width):
    count = lax.axis_size(axis)
    ends = count - 1
    head = lax.slice_in_dim(cells, 0, width, axis=dim)
    tail = lax.slice_in_dim(cells, cells.shape[dim] - width, cells.shape[dim], axis=dim)
    return jnp.concatenate(
        [
            lax.ppermute(tail, axis, [(i, (i + 1) % count) for i in range(ends)]),
            cells,
            lax.ppermute(head, axis, [((i + 1) % count, i) for i in range(ends)]),
        ],
        axis=dim,
    )


def norm_columns(stream, gain):
    average = jnp.mean(stream, 0, keepdims=True)
    centred = stream - average
    variance = jnp.mean(centred * centred, 0, keepdims=True)
    return (centred * lax.rsqrt(variance + 1e-05) * gain).astype(jnp.bfloat16)


def dot(left, right):
    return jnp.dot(left, right, preferred_element_type=jnp.float32)


def dot_first(left, right):
    return lax.dot_general(left, right, (((0,), (0,)), ((), ())), preferred_element_type=jnp.float32)


def flipped(weight):
    return weight.astype(jnp.float32).T.astype(jnp.bfloat16)


def kernel(
    sizes,
    place,
    patches,
    bias,
    opening,
    opening_bias,
    following,
    gains,
    qkv,
    out_weight,
    up,
    down,
    readout,
    result,
    first,
    qkv_t,
    out_t,
    up_t,
    down_t,
    triple,
    attended,
):
    members, row_count, col_count, col_span, row_total, col_total = sizes
    width = opening.shape[2]
    head = width // HEADS
    lanes = patches.shape[2]
    step = pl.program_id(0)

    @pl.when(step == 0)
    def _():
        for layer in range(LAYERS):
            qkv_t[layer] = flipped(qkv[layer])
            out_t[layer] = flipped(out_weight[layer])
            up_t[layer] = flipped(up[layer])
            down_t[layer] = flipped(down[layer])
        chunk = next(c for c in (384, 256, 128) if lanes % c == 0)
        for row in range(row_count + 2):
            row_id = place[0] - 1 + row
            row_fits = (row_id >= 0) & (row_id < row_total)

            def widen(i, carry):
                start = pl.multiple_of(i * chunk, chunk)
                total = jnp.zeros((chunk, width), jnp.float32) + opening_bias[...]
                for off in range(3):
                    total = total + dot_first(patches[row + off, :, pl.ds(start, chunk)], opening[off])
                col_id = place[1] - 1 + (start + lax.broadcasted_iota(jnp.int32, total.shape, 0)) // members
                fits = (col_id >= 0) & (col_id < col_total) & row_fits
                value = jnp.where(fits, jax.nn.gelu(total), 0.0)
                first[pl.ds(pl.multiple_of(row * lanes + start, 128), chunk), :] = value.astype(jnp.bfloat16)
                return carry

            lax.fori_loop(0, lanes // chunk, widen, 0)

    cells = BLOCK // members
    row = (step * cells) // col_count
    col = (step * cells) % col_count

    def shifted(row_off, col_off):
        start = ((row + row_off) * col_span + col + col_off) * members
        return first[pl.ds(pl.multiple_of(start, members), BLOCK), :]

    features = shifted(1, 1).astype(jnp.float32)
    summed = jnp.zeros((BLOCK, width), jnp.float32)
    for tap in range(9):
        summed = summed + dot(shifted(tap // 3, tap % 3), following[tap])
    stream = (features + summed).astype(jnp.bfloat16).astype(jnp.float32).T

    each = LANES // members
    owner = lax.broadcasted_iota(jnp.int32, (members, LANES), 1) // members
    holds = [owner == c for c in range(each)]
    keeps = [jnp.where(hold, 1.0, 0.0).astype(jnp.bfloat16) for hold in holds]
    scale = 1.0 / math.sqrt(head)
    for layer in range(LAYERS):
        normed = norm_columns(stream, gains[:, 2 * layer : 2 * layer + 1])
        triple[...] = dot(qkv_t[layer], normed).astype(jnp.bfloat16)
        for group in range(BLOCK // LANES):
            at = slice(group * LANES, (group + 1) * LANES)
            offset = bias[group].astype(jnp.float32)
            for h in range(HEADS):
                rows = slice(h * head, (h + 1) * head)
                queries = triple[h * head : (h + 1) * head, at]
                keys = triple[width + h * head : width + (h + 1) * head, at]
                values = triple[2 * width + h * head : 2 * width + (h + 1) * head, at]
                every = dot_first(keys, queries)
                scores = every[:members]
                for c in range(1, each):
                    scores = jnp.where(holds[c], every[c * members : (c + 1) * members], scores)
                scores = scores * scale + offset
                raised = jnp.exp(scores - jnp.max(scores, 0, keepdims=True))
                weights = (raised * (1.0 / jnp.sum(raised, 0, keepdims=True))).astype(jnp.bfloat16)
                spread = jnp.concatenate([weights * keep for keep in keeps], axis=0)
                attended[rows, at] = dot(values, spread).astype(jnp.bfloat16)
        stream = stream + dot(out_t[layer], attended[...])
        normed = norm_columns(stream, gains[:, 2 * layer + 1 : 2 * layer + 2])
        hidden = jax.nn.gelu(dot(up_t[layer], normed)).astype(jnp.bfloat16)
        stream = stream + dot(down_t[layer], hidden)
    final = norm_columns(stream, gains[:, 2 * LAYERS : 2 * LAYERS + 1])
    result[...] = dot(readout[...], final)[: result.shape[0]]


def shards(
    member_predictors,
    member_skill_logit,
    opening_filter,
    opening_bias,
    following_filter,
    layer_norm_scales,
    query_key_value_weight,
    attention_output_weight,
    upward_weight,
    downward_weight,
    closing_norm_scale,
    readout_weight,
):
    held, fields, row_span, col_total = member_predictors.shape
    groups = lax.axis_size("mem")
    members = held * groups
    cols = col_total // groups
    row_total = row_span * lax.axis_size("sp")
    width = opening_filter.shape[2]
    place = jnp.stack([lax.axis_index("sp") * row_span, lax.axis_index("mem") * cols]).astype(jnp.int32)

    padded = extended(member_predictors, "sp", 2, 2)
    padded = jnp.pad(padded, ((0, 0), (0, 0), (0, 0), (2, 2)))
    parcels = jnp.stack(
        [
            jnp.concatenate(
                [
                    padded[:, :, :, k * cols : (k + 1) * cols + 4].reshape(held, -1),
                    member_skill_logit[:, :, k * cols : (k + 1) * cols].reshape(held, -1),
                ],
                axis=1,
            )
            for k in range(groups)
        ]
    )
    parcels = lax.all_to_all(parcels, "mem", split_axis=0, concat_axis=0, tiled=True)
    parcels = parcels.reshape(members, -1)
    rows = row_span + 4
    cut = fields * rows * (cols + 4)
    local = parcels[:, :cut].reshape(members, fields, rows, cols + 4)
    logits = parcels[:, cut:].reshape(members, row_span * cols)

    lanes = -(-(cols + 2) * members // LANES) * LANES
    col_span = lanes // members
    local = local.transpose(2, 1, 3, 0).reshape(rows, fields, (cols + 4) * members)
    local = jnp.pad(local, ((0, 0), (0, 0), (0, max(0, lanes - (cols + 2) * members))))
    patches = jnp.concatenate(
        [local[:, :, off * members : off * members + lanes] for off in range(3)], axis=1
    )
    opening = opening_filter.reshape(3, 3 * fields, width)
    each = LANES // members
    bias = logits.reshape(members, -1, each).transpose(1, 0, 2)
    bias = jnp.repeat(bias, members, axis=2)
    gains = jnp.concatenate(
        [layer_norm_scales.reshape(2 * LAYERS, width), closing_norm_scale[None]], axis=0
    )
    gains = jnp.pad(gains, ((0, 8 - gains.shape[0]), (0, 0))).T
    readout = jnp.pad(readout_weight.T, ((0, 16 - readout_weight.shape[1]), (0, 0)))

    tokens = row_span * cols * members
    sizes = (members, row_span, cols, col_span, row_total, col_total)
    whole = pl.BlockSpec(memory_space=pltpu.VMEM)
    ff = upward_weight.shape[2]
    correction = pl.pallas_call(
        functools.partial(kernel, sizes),
        grid=(tokens // BLOCK,),
        out_shape=jax.ShapeDtypeStruct((CORRECTED_COUNT, tokens), jnp.float32),
        in_specs=[
            pl.BlockSpec(memory_space=pltpu.SMEM),
            whole,
            pl.BlockSpec((BLOCK // LANES, members, LANES), lambda i: (i, 0, 0)),
        ]
        + [whole] * 9,
        out_specs=pl.BlockSpec((CORRECTED_COUNT, BLOCK), lambda i: (0, i)),
        scratch_shapes=[
            pltpu.VMEM(((row_span + 2) * lanes, width), jnp.bfloat16),
            pltpu.VMEM((LAYERS, 3 * width, width), jnp.bfloat16),
            pltpu.VMEM((LAYERS, width, width), jnp.bfloat16),
            pltpu.VMEM((LAYERS, ff, width), jnp.bfloat16),
            pltpu.VMEM((LAYERS, width, ff), jnp.bfloat16),
            pltpu.VMEM((3 * width, BLOCK), jnp.bfloat16),
            pltpu.VMEM((width, BLOCK), jnp.bfloat16),
        ],
        compiler_params=pltpu.CompilerParams(dimension_semantics=("arbitrary",)),
        name="members_attend",
    )(
        place,
        patches,
        bias,
        opening,
        opening_bias[None],
        following_filter,
        gains,
        query_key_value_weight,
        attention_output_weight,
        upward_weight,
        downward_weight,
        readout,
    )
    correction = correction.reshape(CORRECTED_COUNT, row_span, cols, members).transpose(3, 0, 1, 2)
    correction = lax.all_to_all(correction, "mem", split_axis=0, concat_axis=3, tiled=True)
    return member_predictors[:, :CORRECTED_COUNT].astype(jnp.float32) + correction


def solution(mesh):
    in_specs = (P("mem", None, "sp", None), P("mem", "sp", None)) + (P(),) * 10
    out_specs = P("mem", None, "sp", None)
    return jax.shard_map(shards, mesh=mesh, in_specs=in_specs, out_specs=out_specs, check_vma=False)
```

```python
import functools
import math

import jax
import jax.numpy as jnp
from jax import lax
from jax.experimental import pallas as pl
from jax.experimental.pallas import tpu as pltpu
from jax.sharding import PartitionSpec as P

CORRECTED_COUNT = 2
HEADS = 8
LAYERS = 2
LANES = 128
BLOCK = 256


def extended(cells, axis, dim, width):
    count = lax.axis_size(axis)
    ends = count - 1
    head = lax.slice_in_dim(cells, 0, width, axis=dim)
    tail = lax.slice_in_dim(cells, cells.shape[dim] - width, cells.shape[dim], axis=dim)
    return jnp.concatenate(
        [
            lax.ppermute(tail, axis, [(i, (i + 1) % count) for i in range(ends)]),
            cells,
            lax.ppermute(head, axis, [((i + 1) % count, i) for i in range(ends)]),
        ],
        axis=dim,
    )


def norm_columns(stream, gain):
    average = jnp.mean(stream, 0, keepdims=True)
    centred = stream - average
    variance = jnp.mean(centred * centred, 0, keepdims=True)
    return (centred * lax.rsqrt(variance + 1e-05) * gain).astype(jnp.bfloat16)


def dot(left, right):
    return jnp.dot(left, right, preferred_element_type=jnp.float32)


def dot_first(left, right):
    return lax.dot_general(left, right, (((0,), (0,)), ((), ())), preferred_element_type=jnp.float32)


def flipped(weight):
    return weight.astype(jnp.float32).T.astype(jnp.bfloat16)


def kernel(
    sizes,
    place,
    patches,
    bias,
    opening,
    opening_bias,
    following,
    gains,
    qkv,
    out_weight,
    up,
    down,
    readout,
    result,
    first,
    qkv_t,
    out_t,
    up_t,
    down_t,
    triple,
    attended,
):
    members, row_count, col_count, col_span, row_total, col_total = sizes
    width = opening.shape[2]
    head = width // HEADS
    lanes = patches.shape[2]
    step = pl.program_id(0)

    @pl.when(step == 0)
    def _():
        for layer in range(LAYERS):
            qkv_t[layer] = flipped(qkv[layer])
            out_t[layer] = flipped(out_weight[layer])
            up_t[layer] = flipped(up[layer])
            down_t[layer] = flipped(down[layer])
        chunk = next(c for c in (384, 256, 128) if lanes % c == 0)
        for row in range(row_count + 2):
            row_id = place[0] - 1 + row
            row_fits = (row_id >= 0) & (row_id < row_total)

            def widen(i, carry):
                start = pl.multiple_of(i * chunk, chunk)
                total = jnp.zeros((chunk, width), jnp.float32) + opening_bias[...]
                for off in range(3):
                    total = total + dot_first(patches[row + off, :, pl.ds(start, chunk)], opening[off])
                spot = start + lax.broadcasted_iota(jnp.int32, (chunk, 1), 0)
                fits = (spot >= (1 - place[1]) * members) & (spot < (col_total + 1 - place[1]) * members)
                fits = fits & row_fits
                value = jnp.where(fits, jax.nn.gelu(total), 0.0)
                first[pl.ds(pl.multiple_of(row * lanes + start, 128), chunk), :] = value.astype(jnp.bfloat16)
                return carry

            lax.fori_loop(0, lanes // chunk, widen, 0)

    cells = BLOCK // members
    row = (step * cells) // col_count
    col = (step * cells) % col_count

    def shifted(row_off, col_off):
        start = ((row + row_off) * col_span + col + col_off) * members
        return first[pl.ds(pl.multiple_of(start, members), BLOCK), :]

    features = shifted(1, 1).astype(jnp.float32)
    summed = jnp.zeros((BLOCK, width), jnp.float32)
    for tap in range(9):
        summed = summed + dot(shifted(tap // 3, tap % 3), following[tap])
    stream = (features + summed).astype(jnp.bfloat16).astype(jnp.float32).T

    each = LANES // members
    lane = lax.broadcasted_iota(jnp.int32, (members, LANES), 1)
    holds = [(lane >= c * members) & (lane < (c + 1) * members) for c in range(each)]
    keeps = [jnp.where(hold, 1.0, 0.0).astype(jnp.bfloat16) for hold in holds]
    scale = 1.0 / math.sqrt(head)
    for layer in range(LAYERS):
        normed = norm_columns(stream, gains[:, 2 * layer : 2 * layer + 1])
        triple[...] = dot(qkv_t[layer], normed).astype(jnp.bfloat16)
        units = [
            (group, slice(group * LANES, (group + 1) * LANES), h * head)
            for group in range(BLOCK // LANES)
            for h in range(HEADS)
        ]
        every = [
            dot_first(triple[width + low : width + low + head, at], triple[low : low + head, at])
            for _, at, low in units
        ]
        scores = []
        for (group, at, low), square in zip(units, every):
            kept = square[:members]
            for c in range(1, each):
                kept = jnp.where(holds[c], square[c * members : (c + 1) * members], kept)
            scores.append(kept * scale + bias[group].astype(jnp.float32))
        highest = [jnp.max(kept, 0, keepdims=True) for kept in scores]
        raised = [jnp.exp(kept - top) for kept, top in zip(scores, highest)]
        shares = [1.0 / jnp.sum(value, 0, keepdims=True) for value in raised]
        weights = [(value * share).astype(jnp.bfloat16) for value, share in zip(raised, shares)]
        for (group, at, low), weight in zip(units, weights):
            spread = jnp.concatenate([weight * keep for keep in keeps], axis=0)
            values = triple[2 * width + low : 2 * width + low + head, at]
            attended[low : low + head, at] = dot(values, spread).astype(jnp.bfloat16)
        stream = stream + dot(out_t[layer], attended[...])
        normed = norm_columns(stream, gains[:, 2 * layer + 1 : 2 * layer + 2])
        hidden = jax.nn.gelu(dot(up_t[layer], normed)).astype(jnp.bfloat16)
        stream = stream + dot(down_t[layer], hidden)
    final = norm_columns(stream, gains[:, 2 * LAYERS : 2 * LAYERS + 1])
    result[...] = dot(readout[...], final)[: result.shape[0]]


def shards(
    member_predictors,
    member_skill_logit,
    opening_filter,
    opening_bias,
    following_filter,
    layer_norm_scales,
    query_key_value_weight,
    attention_output_weight,
    upward_weight,
    downward_weight,
    closing_norm_scale,
    readout_weight,
):
    held, fields, row_span, col_total = member_predictors.shape
    groups = lax.axis_size("mem")
    members = held * groups
    cols = col_total // groups
    row_total = row_span * lax.axis_size("sp")
    width = opening_filter.shape[2]
    place = jnp.stack([lax.axis_index("sp") * row_span, lax.axis_index("mem") * cols]).astype(jnp.int32)

    padded = extended(member_predictors, "sp", 2, 2)
    padded = jnp.pad(padded, ((0, 0), (0, 0), (0, 0), (2, 2)))
    parcels = jnp.stack(
        [
            jnp.concatenate(
                [
                    padded[:, :, :, k * cols : (k + 1) * cols + 4].reshape(held, -1),
                    member_skill_logit[:, :, k * cols : (k + 1) * cols].reshape(held, -1),
                ],
                axis=1,
            )
            for k in range(groups)
        ]
    )
    parcels = lax.all_to_all(parcels, "mem", split_axis=0, concat_axis=0, tiled=True)
    parcels = parcels.reshape(members, -1)
    rows = row_span + 4
    cut = fields * rows * (cols + 4)
    local = parcels[:, :cut].reshape(members, fields, rows, cols + 4)
    logits = parcels[:, cut:].reshape(members, row_span * cols)

    lanes = -(-(cols + 2) * members // LANES) * LANES
    col_span = lanes // members
    local = local.transpose(2, 1, 3, 0).reshape(rows, fields, (cols + 4) * members)
    local = jnp.pad(local, ((0, 0), (0, 0), (0, max(0, lanes - (cols + 2) * members))))
    patches = jnp.concatenate(
        [local[:, :, off * members : off * members + lanes] for off in range(3)], axis=1
    )
    opening = opening_filter.reshape(3, 3 * fields, width)
    each = LANES // members
    bias = logits.reshape(members, -1, each).transpose(1, 0, 2)
    bias = jnp.repeat(bias, members, axis=2)
    gains = jnp.concatenate(
        [layer_norm_scales.reshape(2 * LAYERS, width), closing_norm_scale[None]], axis=0
    )
    gains = jnp.pad(gains, ((0, 8 - gains.shape[0]), (0, 0))).T
    readout = jnp.pad(readout_weight.T, ((0, 16 - readout_weight.shape[1]), (0, 0)))

    tokens = row_span * cols * members
    sizes = (members, row_span, cols, col_span, row_total, col_total)
    whole = pl.BlockSpec(memory_space=pltpu.VMEM)
    ff = upward_weight.shape[2]
    correction = pl.pallas_call(
        functools.partial(kernel, sizes),
        grid=(tokens // BLOCK,),
        out_shape=jax.ShapeDtypeStruct((CORRECTED_COUNT, tokens), jnp.float32),
        in_specs=[
            pl.BlockSpec(memory_space=pltpu.SMEM),
            whole,
            pl.BlockSpec((BLOCK // LANES, members, LANES), lambda i: (i, 0, 0)),
        ]
        + [whole] * 9,
        out_specs=pl.BlockSpec((CORRECTED_COUNT, BLOCK), lambda i: (0, i)),
        scratch_shapes=[
            pltpu.VMEM(((row_span + 2) * lanes, width), jnp.bfloat16),
            pltpu.VMEM((LAYERS, 3 * width, width), jnp.bfloat16),
            pltpu.VMEM((LAYERS, width, width), jnp.bfloat16),
            pltpu.VMEM((LAYERS, ff, width), jnp.bfloat16),
            pltpu.VMEM((LAYERS, width, ff), jnp.bfloat16),
            pltpu.VMEM((3 * width, BLOCK), jnp.bfloat16),
            pltpu.VMEM((width, BLOCK), jnp.bfloat16),
        ],
        compiler_params=pltpu.CompilerParams(dimension_semantics=("arbitrary",)),
        name="members_attend",
    )(
        place,
        patches,
        bias,
        opening,
        opening_bias[None],
        following_filter,
        gains,
        query_key_value_weight,
        attention_output_weight,
        upward_weight,
        downward_weight,
        readout,
    )
    correction = correction.reshape(CORRECTED_COUNT, row_span, cols, members).transpose(3, 0, 1, 2)
    correction = lax.all_to_all(correction, "mem", split_axis=0, concat_axis=3, tiled=True)
    return member_predictors[:, :CORRECTED_COUNT].astype(jnp.float32) + correction


def solution(mesh):
    in_specs = (P("mem", None, "sp", None), P("mem", "sp", None)) + (P(),) * 10
    out_specs = P("mem", None, "sp", None)
    return jax.shard_map(shards, mesh=mesh, in_specs=in_specs, out_specs=out_specs, check_vma=False)
```

```python
import functools
import math

import jax
import jax.numpy as jnp
from jax import lax
from jax.experimental import pallas as pl
from jax.experimental.pallas import tpu as pltpu
from jax.sharding import PartitionSpec as P

CORRECTED_COUNT = 2
HEADS = 8
LAYERS = 2
LANES = 128
BLOCK = 512


def extended(cells, axis, dim, width):
    count = lax.axis_size(axis)
    ends = count - 1
    head = lax.slice_in_dim(cells, 0, width, axis=dim)
    tail = lax.slice_in_dim(cells, cells.shape[dim] - width, cells.shape[dim], axis=dim)
    return jnp.concatenate(
        [
            lax.ppermute(tail, axis, [(i, (i + 1) % count) for i in range(ends)]),
            cells,
            lax.ppermute(head, axis, [((i + 1) % count, i) for i in range(ends)]),
        ],
        axis=dim,
    )


def norm_columns(stream, gain):
    average = jnp.mean(stream, 0, keepdims=True)
    centred = stream - average
    variance = jnp.mean(centred * centred, 0, keepdims=True)
    return (centred * lax.rsqrt(variance + 1e-05) * gain).astype(jnp.bfloat16)


def dot(left, right):
    return jnp.dot(left, right, preferred_element_type=jnp.float32)


def dot_first(left, right):
    return lax.dot_general(left, right, (((0,), (0,)), ((), ())), preferred_element_type=jnp.float32)


def flipped(weight):
    return weight.astype(jnp.float32).T.astype(jnp.bfloat16)


def kernel(
    sizes,
    place,
    patches,
    bias,
    opening,
    opening_bias,
    following,
    gains,
    qkv,
    out_weight,
    up,
    down,
    readout,
    result,
    first,
    qkv_t,
    out_t,
    up_t,
    down_t,
    triple,
    attended,
):
    members, row_count, col_count, col_span, row_total, col_total = sizes
    width = opening.shape[2]
    head = width // HEADS
    lanes = patches.shape[2]
    step = pl.program_id(0)

    @pl.when(step == 0)
    def _():
        for layer in range(LAYERS):
            qkv_t[layer] = flipped(qkv[layer])
            out_t[layer] = flipped(out_weight[layer])
            up_t[layer] = flipped(up[layer])
            down_t[layer] = flipped(down[layer])
        chunk = next(c for c in (384, 256, 128) if lanes % c == 0)
        for row in range(row_count + 2):
            row_id = place[0] - 1 + row
            row_fits = (row_id >= 0) & (row_id < row_total)

            def widen(i, carry):
                start = pl.multiple_of(i * chunk, chunk)
                total = jnp.zeros((chunk, width), jnp.float32) + opening_bias[...]
                for off in range(3):
                    total = total + dot_first(patches[row + off, :, pl.ds(start, chunk)], opening[off])
                spot = start + lax.broadcasted_iota(jnp.int32, (chunk, 1), 0)
                fits = (spot >= (1 - place[1]) * members) & (spot < (col_total + 1 - place[1]) * members)
                fits = fits & row_fits
                value = jnp.where(fits, jax.nn.gelu(total), 0.0)
                first[pl.ds(pl.multiple_of(row * lanes + start, 128), chunk), :] = value.astype(jnp.bfloat16)
                return carry

            lax.fori_loop(0, lanes // chunk, widen, 0)

    cells = BLOCK // members
    row = (step * cells) // col_count
    col = (step * cells) % col_count

    def shifted(row_off, col_off):
        start = ((row + row_off) * col_span + col + col_off) * members
        return first[pl.ds(pl.multiple_of(start, members), BLOCK), :]

    features = shifted(1, 1).astype(jnp.float32)
    taps = jnp.concatenate([shifted(tap // 3, tap % 3) for tap in range(9)], axis=1)
    summed = dot(taps, following[...])
    stream = (features + summed).astype(jnp.bfloat16).astype(jnp.float32).T

    each = LANES // members
    lane = lax.broadcasted_iota(jnp.int32, (members, LANES), 1)
    holds = [(lane >= c * members) & (lane < (c + 1) * members) for c in range(each)]
    keeps = [jnp.where(hold, 1.0, 0.0).astype(jnp.bfloat16) for hold in holds]
    scale = 1.0 / math.sqrt(head)
    for layer in range(LAYERS):
        normed = norm_columns(stream, gains[:, 2 * layer : 2 * layer + 1])
        triple[...] = dot(qkv_t[layer], normed).astype(jnp.bfloat16)
        units = [
            (group, slice(group * LANES, (group + 1) * LANES), h * head)
            for group in range(BLOCK // LANES)
            for h in range(HEADS)
        ]
        every = [
            dot_first(triple[width + low : width + low + head, at], triple[low : low + head, at])
            for _, at, low in units
        ]
        scores = []
        for (group, at, low), square in zip(units, every):
            kept = square[:members]
            for c in range(1, each):
                kept = jnp.where(holds[c], square[c * members : (c + 1) * members], kept)
            scores.append(kept * scale + bias[group].astype(jnp.float32))
        highest = [jnp.max(kept, 0, keepdims=True) for kept in scores]
        raised = [jnp.exp(kept - top) for kept, top in zip(scores, highest)]
        shares = [1.0 / jnp.sum(value, 0, keepdims=True) for value in raised]
        weights = [(value * share).astype(jnp.bfloat16) for value, share in zip(raised, shares)]
        for (group, at, low), weight in zip(units, weights):
            spread = jnp.concatenate([weight * keep for keep in keeps], axis=0)
            values = triple[2 * width + low : 2 * width + low + head, at]
            attended[low : low + head, at] = dot(values, spread).astype(jnp.bfloat16)
        stream = stream + dot(out_t[layer], attended[...])
        normed = norm_columns(stream, gains[:, 2 * layer + 1 : 2 * layer + 2])
        hidden = jax.nn.gelu(dot(up_t[layer], normed)).astype(jnp.bfloat16)
        stream = stream + dot(down_t[layer], hidden)
    final = norm_columns(stream, gains[:, 2 * LAYERS : 2 * LAYERS + 1])
    result[...] = dot(readout[...], final)[: result.shape[0]]


def shards(
    member_predictors,
    member_skill_logit,
    opening_filter,
    opening_bias,
    following_filter,
    layer_norm_scales,
    query_key_value_weight,
    attention_output_weight,
    upward_weight,
    downward_weight,
    closing_norm_scale,
    readout_weight,
):
    held, fields, row_span, col_total = member_predictors.shape
    groups = lax.axis_size("mem")
    members = held * groups
    cols = col_total // groups
    row_total = row_span * lax.axis_size("sp")
    width = opening_filter.shape[2]
    place = jnp.stack([lax.axis_index("sp") * row_span, lax.axis_index("mem") * cols]).astype(jnp.int32)

    padded = extended(member_predictors, "sp", 2, 2)
    padded = jnp.pad(padded, ((0, 0), (0, 0), (0, 0), (2, 2)))
    parcels = jnp.stack(
        [
            jnp.concatenate(
                [
                    padded[:, :, :, k * cols : (k + 1) * cols + 4].reshape(held, -1),
                    member_skill_logit[:, :, k * cols : (k + 1) * cols].reshape(held, -1),
                ],
                axis=1,
            )
            for k in range(groups)
        ]
    )
    parcels = lax.all_to_all(parcels, "mem", split_axis=0, concat_axis=0, tiled=True)
    parcels = parcels.reshape(members, -1)
    rows = row_span + 4
    cut = fields * rows * (cols + 4)
    local = parcels[:, :cut].reshape(members, fields, rows, cols + 4)
    logits = parcels[:, cut:].reshape(members, row_span * cols)

    lanes = -(-(cols + 2) * members // LANES) * LANES
    col_span = lanes // members
    local = local.transpose(2, 1, 3, 0).reshape(rows, fields, (cols + 4) * members)
    local = jnp.pad(local, ((0, 0), (0, 0), (0, max(0, lanes - (cols + 2) * members))))
    patches = jnp.concatenate(
        [local[:, :, off * members : off * members + lanes] for off in range(3)], axis=1
    )
    opening = opening_filter.reshape(3, 3 * fields, width)
    each = LANES // members
    bias = logits.reshape(members, -1, each).transpose(1, 0, 2)
    bias = jnp.repeat(bias, members, axis=2)
    gains = jnp.concatenate(
        [layer_norm_scales.reshape(2 * LAYERS, width), closing_norm_scale[None]], axis=0
    )
    gains = jnp.pad(gains, ((0, 8 - gains.shape[0]), (0, 0))).T
    readout = jnp.pad(readout_weight.T, ((0, 16 - readout_weight.shape[1]), (0, 0)))

    tokens = row_span * cols * members
    sizes = (members, row_span, cols, col_span, row_total, col_total)
    whole = pl.BlockSpec(memory_space=pltpu.VMEM)
    ff = upward_weight.shape[2]
    correction = pl.pallas_call(
        functools.partial(kernel, sizes),
        grid=(tokens // BLOCK,),
        out_shape=jax.ShapeDtypeStruct((CORRECTED_COUNT, tokens), jnp.float32),
        in_specs=[
            pl.BlockSpec(memory_space=pltpu.SMEM),
            whole,
            pl.BlockSpec((BLOCK // LANES, members, LANES), lambda i: (i, 0, 0)),
        ]
        + [whole] * 9,
        out_specs=pl.BlockSpec((CORRECTED_COUNT, BLOCK), lambda i: (0, i)),
        scratch_shapes=[
            pltpu.VMEM(((row_span + 2) * lanes, width), jnp.bfloat16),
            pltpu.VMEM((LAYERS, 3 * width, width), jnp.bfloat16),
            pltpu.VMEM((LAYERS, width, width), jnp.bfloat16),
            pltpu.VMEM((LAYERS, ff, width), jnp.bfloat16),
            pltpu.VMEM((LAYERS, width, ff), jnp.bfloat16),
            pltpu.VMEM((3 * width, BLOCK), jnp.bfloat16),
            pltpu.VMEM((width, BLOCK), jnp.bfloat16),
        ],
        compiler_params=pltpu.CompilerParams(dimension_semantics=("arbitrary",)),
        name="members_attend",
    )(
        place,
        patches,
        bias,
        opening,
        opening_bias[None],
        following_filter.reshape(9 * width, width),
        gains,
        query_key_value_weight,
        attention_output_weight,
        upward_weight,
        downward_weight,
        readout,
    )
    correction = correction.reshape(CORRECTED_COUNT, row_span, cols, members).transpose(3, 0, 1, 2)
    correction = lax.all_to_all(correction, "mem", split_axis=0, concat_axis=3, tiled=True)
    return member_predictors[:, :CORRECTED_COUNT].astype(jnp.float32) + correction


def solution(mesh):
    in_specs = (P("mem", None, "sp", None), P("mem", "sp", None)) + (P(),) * 10
    out_specs = P("mem", None, "sp", None)
    return jax.shard_map(shards, mesh=mesh, in_specs=in_specs, out_specs=out_specs, check_vma=False)
```
